32 devices in a mesh: col: 8 (over y, x, core), row: 4 (over z).
Axes of the slice: x: 2, y: 2, z: 4, core: 2. Of those that a mesh axis runs over, the one named last changes fastest.
Arguments:
- rhs: bfloat16 [6, 8, 4, 128, 512], P(None, 'col', 'row'), may hold values from -6 to 6
- diag_inv: bfloat16 [6, 8, 4, 128, 128], P(None, 'col', 'row'), may hold values from -0.5 to 0.5
- factor: bfloat16 [5, 8, 4, 8, 2, 128, 128], P(None, 'col', 'row'), may hold values from -0.1875 to 0.1875
- columns: int32 [5, 8, 4, 8, 2], P(None, 'col', 'row'), may hold values from 0 to 3, as said below
Outputs:
- solution: bfloat16 [6, 8, 4, 128, 512], P(None, 'col', 'row')
The draws below stay inside these ranges and needn't reach their ends.
Inputs may be any that keep to these rules, and one draw needn't show every extreme that they name: The 2 entries of columns for one factor row block and one column owner are distinct.
All inputs are finite; a program needn't handle non-finite values.
Results may differ from the reference program's by a relative error of at most 0.025.
Values may be sent and summed in bfloat16 or wider, within the bound.
A program may use at most 128 MiB of HBM per device.

```python
import jax
import jax.numpy as jnp
from jax import lax

BLK = 128
NRHS = 512
STEPS = 6
SLOTS = 2
N_COL = 8
N_ROW = 4


def draw_columns(key, part):
    shape = (STEPS - 1, N_COL, N_ROW, N_COL, N_ROW)
    scores = jax.random.randint(jax.random.fold_in(key, 17), shape, 0, 1000)
    scores = scores * N_ROW + jnp.arange(N_ROW, dtype=jnp.int32)
    order = jnp.argsort(scores, axis=-1)
    return order[..., :SLOTS].astype(jnp.int32)


def spiked(result, stream_key, source, target, parts, factor):
    owner, partner = [(jnp.arange(result.shape[dim]) // (result.shape[dim] // parts)).reshape([-1 if axis == dim else 1 for axis in range(result.ndim)]) for dim in (source, target)]
    chosen = jax.random.permutation(stream_key, parts)[partner]
    strong = (owner == chosen) | (owner == (partner + parts // 2) % parts)
    return jnp.where(strong, factor * result, result)


def levels(stream_key, dims, shards, low, largest):
    level = 1.0
    for position, parts in shards:
        steps = jax.random.uniform(jax.random.fold_in(jax.random.fold_in(stream_key, 6), position), (parts,), jnp.float32, low / len(shards), largest / len(shards))
        level = level * jnp.repeat(jnp.exp(steps), dims[position] // parts).reshape((-1,) + (1,) * (len(dims) - 1 - position))
    return level


def gaussian(rng, extent, spread, most, split=(), kind=jnp.bfloat16):
    loudness = levels(rng, extent, split, -0.22, 0.18) if split else 1.0
    array = jax.random.normal(rng, extent, jnp.float32) * spread * loudness
    return jnp.minimum(jnp.maximum(array, -most), most).astype(kind)


def bell_draw_with(stream_key, dims, spread, bound, shards, heavy, held_as=jnp.bfloat16):
    entries = spread * jax.random.normal(stream_key, dims, jnp.float32)
    if shards:
        entries = entries * levels(stream_key, dims, shards, -0.22, 0.18)
    return jnp.clip(spiked(entries, jax.random.fold_in(stream_key, 3), *heavy), -bound, bound).astype(held_as)


def setup_inputs(seed: int = 0) -> dict:
    key_of = jax.random.split(jax.random.key(seed), 5)
    return {
        "rhs": gaussian(key_of[0], (STEPS, N_COL, N_ROW, BLK, NRHS), 1.0, 6.0, ((1, 8), (2, 4))),
        "diag_inv": gaussian(key_of[1], (STEPS, N_COL, N_ROW, BLK, BLK), BLK ** -0.5, 0.5, ((1, 8), (2, 4))),
        "factor": bell_draw_with(key_of[2], (STEPS - 1, N_COL, N_ROW, N_COL, SLOTS, BLK, BLK), (N_COL * SLOTS * BLK) ** -0.5, 0.1875, ((1, 8), (2, 4)), (1, 3, 8, 2.0)),
        "columns": draw_columns(jax.random.fold_in(key_of[4], 71), 0),
    }


def reference(rhs, diag_inv, factor, columns):
    highest = lax.Precision.HIGHEST
    remainder = rhs[0].astype(jnp.float32)
    solved = []
    for step_index in range(STEPS):
        current = jnp.einsum('crab,crbn->cran', diag_inv[step_index].astype(jnp.float32), remainder, precision=highest).astype(jnp.bfloat16)
        solved.append(current)
        if step_index + 1 < STEPS:
            def add_owner(carry, inputs):
                blocks, selected, panels = inputs
                chosen = jnp.take(panels, selected, axis=0).astype(jnp.float32)
                part_sum = jnp.einsum('rtmab,rtmbn->rtan', blocks.astype(jnp.float32), chosen, precision=highest)
                rounded = lax.optimization_barrier(part_sum.astype(jnp.bfloat16))
                return carry + rounded.astype(jnp.float32), None

            start_sum = jnp.zeros((N_ROW, N_COL, BLK, NRHS), jnp.float32)
            total, unused = lax.scan(add_owner, start_sum, (factor[step_index], columns[step_index], current))
            remainder = rhs[step_index + 1].astype(jnp.float32) - jnp.transpose(total, (1, 0, 2, 3))
    return jnp.stack(solved)
```

```python
import functools

import jax
import jax.numpy as jnp
from jax import lax
from jax.experimental import pallas as pl
from jax.experimental.pallas import tpu as pltpu
from jax.sharding import PartitionSpec as P

MESH = pl.DeviceIdType.MESH
CHUNKS = 4
LAG = 1


def kernel(n_col, n_row, rhs, diag, fac, cols, cols_hbm, out, *scratch):
    steps, rows, width = rhs.shape[0], rhs.shape[3], rhs.shape[4]
    slots = fac.shape[4]
    chips = n_col // 2
    half = width // 2
    wide = half // CHUNKS
    fold = max(1, 128 // wide)
    tall = rows // fold
    links = steps - 1

    (rv, dv, fv, cp, own, sent, landed, stage,
     in_loc, in_send, in_recv, z_send, z_recv, c_send, c_recv,
     o_loc, o_send, o_recv) = scratch[:18]
    panels = scratch[18:]

    col = lax.axis_index("col")
    row = lax.axis_index("row")
    core = lax.rem(col, 2)
    chip = lax.div(col, 2)
    partner = col + 1 - 2 * core
    mine = pl.ds(pl.multiple_of(core * half, half), half)
    theirs = pl.ds(pl.multiple_of((1 - core) * half, half), half)

    def to(c, r):
        return {"col": c, "row": r}

    def spans(total):
        return [pl.ds(0, 1), pl.ds(1, total - 1)]

    def chip_at(d):
        if chips & (chips - 1):
            return lax.rem(chip + d, chips)
        other, bit = chip, 1
        while bit < chips:
            if d & bit:
                other = other + bit - 2 * bit * lax.rem(lax.div(chip, bit), 2)
            bit *= 2
        return other

    away = sorted(range(1, chips), key=lambda d: -bin(d).count("1"))

    local = {}
    for g in range(2):
        a, b = spans(steps)[g], spans(links)[g]
        local["rhs", g] = pltpu.make_async_copy(rhs.at[a, 0, 0, :, mine], rv.at[a, 0], in_loc.at[0, g])
        local["diag", g] = pltpu.make_async_copy(diag.at[a, 0, 0], dv.at[a, 0], in_loc.at[1, g])
        local["fac", g] = pltpu.make_async_copy(fac.at[b, 0, 0], fv.at[b, 0], in_loc.at[2, g])
    for c in local.values():
        c.start()

    barrier = pltpu.get_barrier_semaphore()
    pl.semaphore_signal(barrier, inc=1, device_id=to(partner, row), device_id_type=MESH)
    for d in range(1, n_row):
        pl.semaphore_signal(barrier, inc=1, device_id=to(col, lax.rem(row + d, n_row)), device_id_type=MESH)
    for d in away:
        pl.semaphore_signal(barrier, inc=1, device_id=to(chip_at(d) * 2 + core, row), device_id_type=MESH)
    pl.semaphore_wait(barrier, n_row + chips - 1)

    def remote(src, dst, send, recv, device):
        return pltpu.make_async_remote_copy(
            src_ref=src, dst_ref=dst, send_sem=send, recv_sem=recv,
            device_id=device, device_id_type=MESH)

    pair = to(partner, row)
    cross = {}
    for g in range(2):
        a, b = spans(steps)[g], spans(links)[g]
        cross["rhs", g] = remote(rhs.at[a, 0, 0, :, theirs], rv.at[a, 1], in_send.at[0, g], in_recv.at[0, g], pair)
        cross["diag", g] = remote(diag.at[a, 0, 0], dv.at[a, 1], in_send.at[1, g], in_recv.at[1, g], pair)
        cross["fac", g] = remote(fac.at[b, 0, 0], fv.at[b, 1], in_send.at[2, g], in_recv.at[2, g], pair)
        if g == 0:
            cross["cols", g] = remote(cols_hbm, cp, in_send.at[3, g], in_recv.at[3, g], pair)
    for c in cross.values():
        c.start()

    def arrived(name, g):
        if (name, g) in local:
            local[name, g].wait()
        cross[name, g].wait_recv()

    def pack(x):
        return x if fold == 1 else jnp.concatenate(
            [x[i * tall:(i + 1) * tall] for i in range(fold)], axis=1)

    def unpack(x):
        return x if fold == 1 else jnp.concatenate(
            [x[:, i * wide:(i + 1) * wide] for i in range(fold)], axis=0)

    def part(ch):
        return pl.ds(ch * wide, wide)

    def z_copy(s, ch, source, target):
        buf = panels[s * CHUNKS + ch].at[source]
        return remote(buf, buf, z_send.at[s % 2, ch], z_recv.at[s % 2, ch, source], to(col, target))

    def z_sent(s, ch):
        many = panels[s * CHUNKS + ch].at[pl.ds(0, n_row - 1)]
        remote(many, many, z_send.at[s % 2, ch], z_recv.at[s % 2, ch, 0], pair).wait_send()

    def z_own(s, ch):
        if s >= 2:
            z_sent(s - 2, ch)
        for d in range(n_row - 1, 0, -1):
            for target in (row + d, row - d):
                ok = (target >= 0) & (target < n_row)

                @pl.when(ok)
                def _():
                    z_copy(s, ch, row, target).start()

    def z_wait(s, ch):
        for d in range(1, n_row):
            for source in (row - d, row + d):
                ok = (source >= 0) & (source < n_row)

                @pl.when(ok)
                def _():
                    z_copy(s, ch, source, row).wait_recv()

    def c_copy(s, ch, d):
        other = chip_at(d) * 2 + core
        return remote(sent.at[s, ch, d - 1], landed.at[s, ch, d - 1], c_send.at[0],
                      c_recv.at[s % 2, ch], to(other, row))

    def c_wait(s, ch):
        remote(sent.at[s, ch], landed.at[s, ch], c_send.at[0], c_recv.at[s % 2, ch], to(col, row)).wait_recv()

    def out_copies(s, ch):
        first, size = (ch + 1 - fold) * wide, fold * wide
        span = pl.ds(pl.multiple_of(core * half + first, size), size)
        src = stage.at[s, :, :, pl.ds(first, size)]
        keep = pltpu.make_async_copy(src.at[0], out.at[s, 0, 0, :, span], o_loc.at[0])
        give = remote(src.at[1], out.at[s, 0, 0, :, span], o_send.at[0], o_recv.at[0], pair)
        return keep, give

    def solve(s, ch):
        if s > 0:
            c_wait(s - 1, ch)
        for k in range(2):
            block = dv[s, k]
            right = rv[s, k, :, part(ch)]
            if s == 0:
                x = jnp.dot(block, right, preferred_element_type=jnp.float32)
            else:
                total = own[ch, k]
                for d in range(1, chips):
                    total = total + unpack(landed[s - 1, ch, d - 1, k]).astype(jnp.float32)
                rem = right.astype(jnp.float32) - total
                high = rem.astype(jnp.bfloat16)
                low = (rem - high.astype(jnp.float32)).astype(jnp.bfloat16)
                x = jnp.dot(jnp.concatenate([block, block], axis=1),
                            jnp.concatenate([high, low], axis=0),
                            preferred_element_type=jnp.float32)
            x = x.astype(jnp.bfloat16)
            if s < links:
                panels[s * CHUNKS + ch][row, k] = pack(x)
            stage[s, k, :, part(ch)] = x
        if s < links:
            z_own(s, ch)
        if ch % fold == fold - 1:
            for c in out_copies(s, ch):
                c.start()

    def term(s, ch, other, k):
        buf = panels[s * CHUNKS + ch]
        t = other * 2 + (core if k == 0 else 1 - core)
        left, right = [], []
        for slot, index in ((0, cols), (1, cp)):
            for m in range(slots):
                left.append(fv[s, slot, t, m])
                right.append(unpack(buf[index[s, 0, 0, m, t], slot]))
        return jnp.dot(jnp.concatenate(left, axis=1), jnp.concatenate(right, axis=0),
                       preferred_element_type=jnp.float32)

    def spread(s, ch):
        z_wait(s, ch)
        for d in away:
            other = chip_at(d)
            for k in range(2):
                sent[s, ch, d - 1, k] = pack(term(s, ch, other, k).astype(jnp.bfloat16))
            c_copy(s, ch, d).start()
        for k in range(2):
            own[ch, k] = term(s, ch, chip, k)

    def ready(s, names):
        if s < 2:
            for name in names:
                arrived(name, s)

    n = CHUNKS

    def do_solve(i):
        s, ch = divmod(i, n)
        if ch == 0:
            ready(s, ("rhs", "diag"))
        solve(s, ch)

    def do_spread(j):
        s, ch = divmod(j, n)
        if ch == 0:
            ready(s, ("fac", "cols") if s == 0 else ("fac",))
        spread(s, ch)

    for i in range(n):
        do_solve(i)
    solved = n
    for j in range(links * n):
        do_spread(j)
        if j + n - LAG >= n:
            do_solve(j + n - LAG)
            solved += 1
    while solved < steps * n:
        do_solve(solved)
        solved += 1

    for c in cross.values():
        c.wait_send()
    pltpu.make_async_copy(stage.at[:, 0], out.at[:, 0, 0, :, mine], o_loc.at[0]).wait()
    give = remote(stage.at[:, 1], out.at[:, 0, 0, :, mine], o_send.at[0], o_recv.at[0], pair)
    give.wait_send()
    give.wait_recv()
    for s in range(max(0, links - 2), links):
        for ch in range(n):
            z_sent(s, ch)
    remote(sent, landed, c_send.at[0], c_recv.at[0, 0], pair).wait_send()


def on_device(n_col, n_row, rhs, diag_inv, factor, columns):
    steps, rows, width = rhs.shape[0], rhs.shape[3], rhs.shape[4]
    columns = jnp.swapaxes(columns, 3, 4)
    targets, slots = factor.shape[3], factor.shape[4]
    chips, half = n_col // 2, width // 2
    wide, links = half // CHUNKS, steps - 1
    fold = max(1, 128 // wide)
    packed = (rows // fold, wide * fold)
    bf16 = jnp.bfloat16
    dma = pltpu.SemaphoreType.DMA
    scratch = [
        pltpu.VMEM((steps, 2, rows, half), bf16),
        pltpu.VMEM((steps, 2, rows, rows), bf16),
        pltpu.VMEM((links, 2, targets, slots, rows, rows), bf16),
        pltpu.SMEM(columns.shape, jnp.int32),
        pltpu.VMEM((CHUNKS, 2, rows, wide), jnp.float32),
        pltpu.VMEM((links, CHUNKS, chips - 1, 2) + packed, bf16),
        pltpu.VMEM((links, CHUNKS, chips - 1, 2) + packed, bf16),
        pltpu.VMEM((steps, 2, rows, half), bf16),
        dma((3, 2)), dma((4, 2)), dma((4, 2)),
        dma((2, CHUNKS)), dma((2, CHUNKS, n_row)),
        dma((1,)), dma((2, CHUNKS)),
        dma((1,)), dma((1,)), dma((1,)),
    ] + [pltpu.VMEM((n_row, 2) + packed, bf16) for _ in range(links * CHUNKS)]
    anywhere = pl.BlockSpec(memory_space=pl.ANY)
    return pl.pallas_call(
        functools.partial(kernel, n_col, n_row),
        out_shape=jax.ShapeDtypeStruct(rhs.shape, bf16),
        in_specs=[anywhere, anywhere, anywhere, pl.BlockSpec(memory_space=pltpu.SMEM), anywhere],
        out_specs=anywhere,
        scratch_shapes=scratch,
        compiler_params=pltpu.CompilerParams(
            collective_id=0, has_side_effects=True, vmem_limit_bytes=60 * 1024 * 1024),
        name="levels",
    )(rhs, diag_inv, factor, columns, columns)


def solution(mesh):
    n_col, n_row = mesh.shape["col"], mesh.shape["row"]
    return jax.shard_map(
        functools.partial(on_device, n_col, n_row),
        mesh=mesh,
        in_specs=(
            P(None, "col", "row", None, None),
            P(None, "col", "row", None, None),
            P(None, "col", "row", None, None, None, None),
            P(None, "col", "row", None, None),
        ),
        out_specs=P(None, "col", "row", None, None),
        check_vma=False,
    )
```

```python
import functools

import jax
import jax.numpy as jnp
from jax import lax
from jax.experimental import pallas as pl
from jax.experimental.pallas import tpu as pltpu
from jax.sharding import PartitionSpec as P

MESH = pl.DeviceIdType.MESH
CHUNKS = 4
LAG = 1


def kernel(n_col, n_row, rhs, diag, fac, cols, cols_hbm, out, *scratch):
    steps, rows, width = rhs.shape[0], rhs.shape[3], rhs.shape[4]
    slots = fac.shape[4]
    chips = n_col // 2
    half = width // 2
    wide = half // CHUNKS
    fold = max(1, 128 // wide)
    tall = rows // fold
    links = steps - 1

    (rv, dv, fv, cp, own, sent, landed, stage,
     in_loc, in_send, in_recv, z_send, z_recv, c_send, c_recv,
     o_loc, o_send, o_recv, first_rhs, first_sol, first_pair) = scratch[:21]
    panels = scratch[21:]

    col = lax.axis_index("col")
    row = lax.axis_index("row")
    core = lax.rem(col, 2)
    chip = lax.div(col, 2)
    partner = col + 1 - 2 * core
    mine = pl.ds(pl.multiple_of(core * half, half), half)
    theirs = pl.ds(pl.multiple_of((1 - core) * half, half), half)

    def to(c, r):
        return {"col": c, "row": r}

    def spans(total):
        return [pl.ds(0, 1), pl.ds(1, total - 1)]

    def chip_at(d):
        if chips & (chips - 1):
            return lax.rem(chip + d, chips)
        other, bit = chip, 1
        while bit < chips:
            if d & bit:
                other = other + bit - 2 * bit * lax.rem(lax.div(chip, bit), 2)
            bit *= 2
        return other

    away = sorted(range(1, chips), key=lambda d: -bin(d).count("1"))

    local = {
        ("rhs", 0): pltpu.make_async_copy(rhs.at[0, 0, 0], first_rhs, in_loc.at[0, 0]),
        ("diag", 0): pltpu.make_async_copy(diag.at[0, 0, 0], dv.at[0, 0], in_loc.at[1, 0]),
    }
    later = pl.ds(1, steps - 1)
    for g in range(2):
        b = spans(links)[g]
        local["fac", g] = pltpu.make_async_copy(fac.at[b, 0, 0], fv.at[b, 0], in_loc.at[2, g])
        if g == 0:
            local["rhs", 1] = pltpu.make_async_copy(rhs.at[later, 0, 0, :, mine], rv.at[later, 0], in_loc.at[0, 1])
            local["diag", 1] = pltpu.make_async_copy(diag.at[later, 0, 0], dv.at[later, 0], in_loc.at[1, 1])
    for c in local.values():
        c.start()

    barrier = pltpu.get_barrier_semaphore()
    pl.semaphore_signal(barrier, inc=1, device_id=to(partner, row), device_id_type=MESH)
    for d in range(1, n_row):
        for c in (col, partner):
            pl.semaphore_signal(barrier, inc=1, device_id=to(c, lax.rem(row + d, n_row)), device_id_type=MESH)
    for d in away:
        pl.semaphore_signal(barrier, inc=1, device_id=to(chip_at(d) * 2 + core, row), device_id_type=MESH)

    def pack(x):
        return x if fold == 1 else jnp.concatenate(
            [x[i * tall:(i + 1) * tall] for i in range(fold)], axis=1)

    local["rhs", 0].wait()
    local["diag", 0].wait()
    first_sol[...] = jnp.dot(dv[0, 0], first_rhs[...], preferred_element_type=jnp.float32).astype(jnp.bfloat16)
    first_out = pltpu.make_async_copy(first_sol, out.at[0, 0, 0], o_loc.at[1])
    first_out.start()
    keep, give = first_sol[:, mine], first_sol[:, theirs]
    for ch in range(CHUNKS):
        panels[ch][row, 0] = pack(keep[:, ch * wide:(ch + 1) * wide])
        first_pair[ch] = pack(give[:, ch * wide:(ch + 1) * wide])
    pl.semaphore_wait(barrier, 2 * n_row + chips - 2)

    def remote(src, dst, send, recv, device):
        return pltpu.make_async_remote_copy(
            src_ref=src, dst_ref=dst, send_sem=send, recv_sem=recv,
            device_id=device, device_id_type=MESH)

    pair = to(partner, row)
    cross = {}
    for g in range(2):
        b = spans(links)[g]
        if g == 0:
            cross["cols", 0] = remote(cols_hbm, cp, in_send.at[3, 0], in_recv.at[3, 0], pair)
        cross["fac", g] = remote(fac.at[b, 0, 0], fv.at[b, 1], in_send.at[2, g], in_recv.at[2, g], pair)
        if g == 0:
            cross["rhs", 1] = remote(rhs.at[later, 0, 0, :, theirs], rv.at[later, 1], in_send.at[0, 1], in_recv.at[0, 1], pair)
            cross["diag", 1] = remote(diag.at[later, 0, 0], dv.at[later, 1], in_send.at[1, 1], in_recv.at[1, 1], pair)

    def first_copy(ch, slot, target):
        buf = panels[ch].at[row, slot]
        if slot == 0:
            return remote(buf, buf, z_send.at[0, ch], z_recv.at[0, ch, row], to(col, target))
        return remote(first_pair.at[ch], buf, z_send.at[0, ch], z_recv.at[0, ch, row], to(partner, target))

    def first_swap(ch):
        return remote(first_pair.at[ch], panels[ch].at[row, 1], z_send.at[1, ch], z_recv.at[0, ch, row], pair)

    for ch in range(CHUNKS):
        for d in range(n_row - 1, 0, -1):
            for target in (row + d, row - d):
                @pl.when((target >= 0) & (target < n_row))
                def _():
                    for slot in range(2):
                        first_copy(ch, slot, target).start()
        first_swap(ch).start()
    for c in cross.values():
        c.start()

    def arrived(name, g):
        if (name, g) in local:
            local[name, g].wait()
        cross[name, g].wait_recv()

    def unpack(x):
        return x if fold == 1 else jnp.concatenate(
            [x[:, i * wide:(i + 1) * wide] for i in range(fold)], axis=0)

    def part(ch):
        return pl.ds(ch * wide, wide)

    def z_copy(s, ch, source, target):
        buf = panels[s * CHUNKS + ch].at[source]
        return remote(buf, buf, z_send.at[s % 2, ch], z_recv.at[s % 2, ch, source], to(col, target))

    def z_sent(s, ch):
        many = panels[s * CHUNKS + ch].at[pl.ds(0, n_row - 1)]
        remote(many, many, z_send.at[s % 2, ch], z_recv.at[s % 2, ch, 0], pair).wait_send()

    def z_own(s, ch):
        if s >= 2:
            z_sent(s - 2, ch)
        else:
            first_swap(ch).wait_send()
        for d in range(n_row - 1, 0, -1):
            for target in (row + d, row - d):
                ok = (target >= 0) & (target < n_row)

                @pl.when(ok)
                def _():
                    z_copy(s, ch, row, target).start()

    def z_wait(s, ch):
        if s == 0:
            first_swap(ch).wait_recv()
        for d in range(1, n_row):
            for source in (row - d, row + d):
                ok = (source >= 0) & (source < n_row)

                @pl.when(ok)
                def _():
                    z_copy(s, ch, source, row).wait_recv()

    def c_copy(s, ch, d):
        other = chip_at(d) * 2 + core
        return remote(sent.at[s, ch, d - 1], landed.at[s, ch, d - 1], c_send.at[0],
                      c_recv.at[s % 2, ch], to(other, row))

    def c_wait(s, ch):
        remote(sent.at[s, ch], landed.at[s, ch], c_send.at[0], c_recv.at[s % 2, ch], to(col, row)).wait_recv()

    def out_copies(s, ch):
        first, size = (ch + 1 - fold) * wide, fold * wide
        span = pl.ds(pl.multiple_of(core * half + first, size), size)
        src = stage.at[s, :, :, pl.ds(first, size)]
        keep = pltpu.make_async_copy(src.at[0], out.at[s, 0, 0, :, span], o_loc.at[0])
        give = remote(src.at[1], out.at[s, 0, 0, :, span], o_send.at[0], o_recv.at[0], pair)
        return keep, give

    def solve(s, ch):
        c_wait(s - 1, ch)
        for k in range(2):
            block = dv[s, k]
            right = rv[s, k, :, part(ch)]
            total = own[ch, k]
            for d in range(1, chips):
                total = total + unpack(landed[s - 1, ch, d - 1, k]).astype(jnp.float32)
            rem = right.astype(jnp.float32) - total
            high = rem.astype(jnp.bfloat16)
            low = (rem - high.astype(jnp.float32)).astype(jnp.bfloat16)
            x = jnp.dot(jnp.concatenate([block, block], axis=1),
                        jnp.concatenate([high, low], axis=0),
                        preferred_element_type=jnp.float32)
            x = x.astype(jnp.bfloat16)
            if s < links:
                panels[s * CHUNKS + ch][row, k] = pack(x)
            stage[s, k, :, part(ch)] = x
        if s < links:
            z_own(s, ch)
        if ch % fold == fold - 1:
            for c in out_copies(s, ch):
                c.start()

    def term(s, ch, other, k):
        buf = panels[s * CHUNKS + ch]
        t = other * 2 + (core if k == 0 else 1 - core)
        left, right = [], []
        for slot, index in ((0, cols), (1, cp)):
            for m in range(slots):
                left.append(fv[s, slot, t, m])
                right.append(unpack(buf[index[s, 0, 0, m, t], slot]))
        return jnp.dot(jnp.concatenate(left, axis=1), jnp.concatenate(right, axis=0),
                       preferred_element_type=jnp.float32)

    def spread(s, ch):
        z_wait(s, ch)
        for d in away:
            other = chip_at(d)
            for k in range(2):
                sent[s, ch, d - 1, k] = pack(term(s, ch, other, k).astype(jnp.bfloat16))
            c_copy(s, ch, d).start()
        for k in range(2):
            own[ch, k] = term(s, ch, chip, k)

    def ready(s, names):
        if s < 2:
            for name in names:
                arrived(name, s)

    n = CHUNKS

    def do_solve(i):
        s, ch = divmod(i, n)
        if ch == 0 and s == 1:
            ready(s, ("rhs", "diag"))
        solve(s, ch)

    def do_spread(j):
        s, ch = divmod(j, n)
        if ch == 0:
            ready(s, ("fac", "cols") if s == 0 else ("fac",))
        spread(s, ch)

    solved = n
    for j in range(links * n):
        do_spread(j)
        if j + n - LAG >= n:
            do_solve(j + n - LAG)
            solved += 1
    while solved < steps * n:
        do_solve(solved)
        solved += 1

    for c in cross.values():
        c.wait_send()
    first_out.wait()
    pltpu.make_async_copy(stage.at[later, 0], out.at[later, 0, 0, :, mine], o_loc.at[0]).wait()
    give = remote(stage.at[later, 1], out.at[later, 0, 0, :, mine], o_send.at[0], o_recv.at[0], pair)
    give.wait_send()
    give.wait_recv()
    for s in range(max(0, links - 2), links):
        for ch in range(n):
            z_sent(s, ch)
    remote(sent, landed, c_send.at[0], c_recv.at[0, 0], pair).wait_send()


def on_device(n_col, n_row, rhs, diag_inv, factor, columns):
    steps, rows, width = rhs.shape[0], rhs.shape[3], rhs.shape[4]
    columns = jnp.swapaxes(columns, 3, 4)
    targets, slots = factor.shape[3], factor.shape[4]
    chips, half = n_col // 2, width // 2
    wide, links = half // CHUNKS, steps - 1
    fold = max(1, 128 // wide)
    packed = (rows // fold, wide * fold)
    bf16 = jnp.bfloat16
    dma = pltpu.SemaphoreType.DMA
    scratch = [
        pltpu.VMEM((steps, 2, rows, half), bf16),
        pltpu.VMEM((steps, 2, rows, rows), bf16),
        pltpu.VMEM((links, 2, targets, slots, rows, rows), bf16),
        pltpu.SMEM(columns.shape, jnp.int32),
        pltpu.VMEM((CHUNKS, 2, rows, wide), jnp.float32),
        pltpu.VMEM((links, CHUNKS, chips - 1, 2) + packed, bf16),
        pltpu.VMEM((links, CHUNKS, chips - 1, 2) + packed, bf16),
        pltpu.VMEM((steps, 2, rows, half), bf16),
        dma((3, 2)), dma((4, 2)), dma((4, 2)),
        dma((2, CHUNKS)), dma((2, CHUNKS, n_row)),
        dma((1,)), dma((2, CHUNKS)),
        dma((2,)), dma((1,)), dma((1,)),
        pltpu.VMEM((rows, width), bf16), pltpu.VMEM((rows, width), bf16), pltpu.VMEM((CHUNKS,) + packed, bf16),
    ] + [pltpu.VMEM((n_row, 2) + packed, bf16) for _ in range(links * CHUNKS)]
    anywhere = pl.BlockSpec(memory_space=pl.ANY)
    return pl.pallas_call(
        functools.partial(kernel, n_col, n_row),
        out_shape=jax.ShapeDtypeStruct(rhs.shape, bf16),
        in_specs=[anywhere, anywhere, anywhere, pl.BlockSpec(memory_space=pltpu.SMEM), anywhere],
        out_specs=anywhere,
        scratch_shapes=scratch,
        compiler_params=pltpu.CompilerParams(
            collective_id=0, has_side_effects=True, vmem_limit_bytes=60 * 1024 * 1024),
        name="levels",
    )(rhs, diag_inv, factor, columns, columns)


def solution(mesh):
    n_col, n_row = mesh.shape["col"], mesh.shape["row"]
    return jax.shard_map(
        functools.partial(on_device, n_col, n_row),
        mesh=mesh,
        in_specs=(
            P(None, "col", "row", None, None),
            P(None, "col", "row", None, None),
            P(None, "col", "row", None, None, None, None),
            P(None, "col", "row", None, None),
        ),
        out_specs=P(None, "col", "row", None, None),
        check_vma=False,
    )
```

```python
import functools

import jax
import jax.numpy as jnp
from jax import lax
from jax.experimental import pallas as pl
from jax.experimental.pallas import tpu as pltpu
from jax.sharding import PartitionSpec as P

MESH = pl.DeviceIdType.MESH
CHUNKS = 4
LAG = 1
HELD = 1


def kernel(n_col, n_row, rhs, diag, fac, cols, cols_hbm, out, *scratch):
    steps, rows, width = rhs.shape[0], rhs.shape[3], rhs.shape[4]
    slots = fac.shape[4]
    chips = n_col // 2
    half = width // 2
    wide = half // CHUNKS
    fold = max(1, 128 // wide)
    tall = rows // fold
    links = steps - 1

    (rv, dv, fv, cp, own, sent, landed, stage,
     in_loc, in_send, in_recv, z_send, z_recv, swapped, c_send, c_recv,
     o_loc, o_send, o_recv, first_rhs, first_sol, first_pair) = scratch[:22]
    panels = scratch[22:]

    col = lax.axis_index("col")
    row = lax.axis_index("row")
    core = lax.rem(col, 2)
    chip = lax.div(col, 2)
    partner = col + 1 - 2 * core
    mine = pl.ds(pl.multiple_of(core * half, half), half)
    theirs = pl.ds(pl.multiple_of((1 - core) * half, half), half)

    def to(c, r):
        return {"col": c, "row": r}

    def spans(total):
        return [pl.ds(0, 1), pl.ds(1, total - 1)]

    def chip_at(d):
        if chips & (chips - 1):
            return lax.rem(chip + d, chips)
        other, bit = chip, 1
        while bit < chips:
            if d & bit:
                other = other + bit - 2 * bit * lax.rem(lax.div(chip, bit), 2)
            bit *= 2
        return other

    away = sorted(range(1, chips), key=lambda d: -bin(d).count("1"))

    barrier = pltpu.get_barrier_semaphore()
    pl.semaphore_signal(barrier, inc=1, device_id=to(partner, row), device_id_type=MESH)
    for d in range(1, n_row):
        for c in (col, partner):
            pl.semaphore_signal(barrier, inc=1, device_id=to(c, lax.rem(row + d, n_row)), device_id_type=MESH)
    for d in away:
        pl.semaphore_signal(barrier, inc=1, device_id=to(chip_at(d) * 2 + core, row), device_id_type=MESH)

    local = {
        ("rhs", 0): pltpu.make_async_copy(rhs.at[0, 0, 0], first_rhs, in_loc.at[0, 0]),
        ("diag", 0): pltpu.make_async_copy(diag.at[0, 0, 0], dv.at[0, 0], in_loc.at[1, 0]),
    }
    later = pl.ds(1, steps - 1)
    for g in range(2):
        b = spans(links)[g]
        local["fac", g] = pltpu.make_async_copy(fac.at[b, 0, 0], fv.at[b, 0], in_loc.at[2, g])
        if g == 0:
            local["rhs", 1] = pltpu.make_async_copy(rhs.at[later, 0, 0, :, mine], rv.at[later, 0], in_loc.at[0, 1])
            local["diag", 1] = pltpu.make_async_copy(diag.at[later, 0, 0], dv.at[later, 0], in_loc.at[1, 1])
    for c in local.values():
        c.start()

    def pack(x):
        return x if fold == 1 else jnp.concatenate(
            [x[i * tall:(i + 1) * tall] for i in range(fold)], axis=1)

    local["rhs", 0].wait()
    local["diag", 0].wait()
    first_sol[...] = jnp.dot(dv[0, 0], first_rhs[...], preferred_element_type=jnp.float32).astype(jnp.bfloat16)
    first_out = pltpu.make_async_copy(first_sol, out.at[0, 0, 0], o_loc.at[1])
    first_out.start()
    keep, give = first_sol[:, mine], first_sol[:, theirs]
    for ch in range(CHUNKS):
        panels[ch][row, 0] = pack(keep[:, ch * wide:(ch + 1) * wide])
        first_pair[ch] = pack(give[:, ch * wide:(ch + 1) * wide])
    pl.semaphore_wait(barrier, 2 * n_row + chips - 2)

    def remote(src, dst, send, recv, device):
        return pltpu.make_async_remote_copy(
            src_ref=src, dst_ref=dst, send_sem=send, recv_sem=recv,
            device_id=device, device_id_type=MESH)

    pair = to(partner, row)
    cross = {}
    for g in range(2):
        b = spans(links)[g]
        if g == 0:
            cross["cols", 0] = remote(cols_hbm, cp, in_send.at[0], in_recv.at[0], pair)
        cross["fac", g] = remote(fac.at[b, 0, 0], fv.at[b, 1], in_send.at[1 + g], in_recv.at[1 + g], pair)
        if g == 0:
            cross["rhs", 1] = remote(rhs.at[later, 0, 0, :, theirs], rv.at[later, 1], in_send.at[3], in_recv.at[3], pair)
            cross["diag", 1] = remote(diag.at[later, 0, 0], dv.at[later, 1], in_send.at[4], in_recv.at[4], pair)

    def first_copy(ch, slot, target):
        buf = panels[ch].at[row, slot]
        if slot == 0:
            return remote(buf, buf, z_send.at[0, ch], z_recv.at[0, ch], to(col, target))
        return remote(first_pair.at[ch], buf, z_send.at[0, ch], z_recv.at[0, ch], to(partner, target))

    def first_swap(ch):
        return remote(first_pair.at[ch], panels[ch].at[row, 1], z_send.at[1, ch], swapped.at[ch], pair)

    def first_send(ch):
        for d in range(n_row - 1, 0, -1):
            for target in (row + d, row - d):
                @pl.when((target >= 0) & (target < n_row))
                def _():
                    for slot in range(2):
                        first_copy(ch, slot, target).start()
        first_swap(ch).start()

    for ch in range(CHUNKS - HELD):
        first_send(ch)
    for c in cross.values():
        c.start()

    def arrived(name, g):
        if (name, g) in local:
            local[name, g].wait()
        cross[name, g].wait_recv()

    def unpack(x):
        return x if fold == 1 else jnp.concatenate(
            [x[:, i * wide:(i + 1) * wide] for i in range(fold)], axis=0)

    def part(ch):
        return pl.ds(ch * wide, wide)

    def z_copy(s, ch, source, target):
        buf = panels[s * CHUNKS + ch].at[source]
        return remote(buf, buf, z_send.at[s % 2, ch], z_recv.at[s % 2, ch], to(col, target))

    def z_sent(s, ch):
        many = panels[s * CHUNKS + ch].at[pl.ds(0, n_row - 1)]
        remote(many, many, z_send.at[s % 2, ch], z_recv.at[s % 2, ch], pair).wait_send()

    def z_own(s, ch):
        if s >= 2:
            z_sent(s - 2, ch)
        if s == 1:
            first_swap(ch).wait_send()
        for d in range(n_row - 1, 0, -1):
            for target in (row + d, row - d):
                ok = (target >= 0) & (target < n_row)

                @pl.when(ok)
                def _():
                    z_copy(s, ch, row, target).start()

    def z_wait(s, ch):
        if s == 0:
            first_swap(ch).wait_recv()
        many = panels[s * CHUNKS + ch].at[pl.ds(0, n_row - 1)]
        remote(many, many, z_send.at[s % 2, ch], z_recv.at[s % 2, ch], pair).wait_recv()

    def c_copy(s, ch, d):
        other = chip_at(d) * 2 + core
        return remote(sent.at[s, ch, d - 1], landed.at[s, ch, d - 1], c_send.at[0],
                      c_recv.at[s % 2, ch], to(other, row))

    def c_wait(s, ch):
        remote(sent.at[s, ch], landed.at[s, ch], c_send.at[0], c_recv.at[s % 2, ch], to(col, row)).wait_recv()

    def out_copies(s, ch):
        first, size = (ch + 1 - fold) * wide, fold * wide
        span = pl.ds(pl.multiple_of(core * half + first, size), size)
        src = stage.at[s, :, :, pl.ds(first, size)]
        keep = pltpu.make_async_copy(src.at[0], out.at[s, 0, 0, :, span], o_loc.at[0])
        give = remote(src.at[1], out.at[s, 0, 0, :, span], o_send.at[0], o_recv.at[0], pair)
        return keep, give

    def solve(s, ch):
        c_wait(s - 1, ch)
        for k in range(2):
            block = dv[s, k]
            right = rv[s, k, :, part(ch)]
            total = own[ch, k]
            for d in range(1, chips):
                total = total + unpack(landed[s - 1, ch, d - 1, k]).astype(jnp.float32)
            rem = right.astype(jnp.float32) - total
            high = rem.astype(jnp.bfloat16)
            low = (rem - high.astype(jnp.float32)).astype(jnp.bfloat16)
            x = jnp.dot(jnp.concatenate([block, block], axis=1),
                        jnp.concatenate([high, low], axis=0),
                        preferred_element_type=jnp.float32)
            x = x.astype(jnp.bfloat16)
            if s < links:
                panels[s * CHUNKS + ch][row, k] = pack(x)
            stage[s, k, :, part(ch)] = x
        if s < links:
            z_own(s, ch)
        if ch % fold == fold - 1:
            for c in out_copies(s, ch):
                c.start()

    def term(s, ch, other, k):
        buf = panels[s * CHUNKS + ch]
        t = other * 2 + (core if k == 0 else 1 - core)
        left, right = [], []
        for slot, index in ((0, cols), (1, cp)):
            for m in range(slots):
                left.append(fv[s, slot, t, m])
                right.append(unpack(buf[index[s, 0, 0, m, t], slot]))
        return jnp.dot(jnp.concatenate(left, axis=1), jnp.concatenate(right, axis=0),
                       preferred_element_type=jnp.float32)

    def spread(s, ch):
        z_wait(s, ch)
        for d in away:
            other = chip_at(d)
            for k in range(2):
                sent[s, ch, d - 1, k] = pack(term(s, ch, other, k).astype(jnp.bfloat16))
            c_copy(s, ch, d).start()
        for k in range(2):
            own[ch, k] = term(s, ch, chip, k)

    def ready(s, names):
        if s < 2:
            for name in names:
                arrived(name, s)

    n = CHUNKS

    def do_solve(i):
        s, ch = divmod(i, n)
        if ch == 0 and s == 1:
            ready(s, ("rhs", "diag"))
        solve(s, ch)

    def do_spread(j):
        s, ch = divmod(j, n)
        if ch == 0:
            ready(s, ("fac", "cols") if s == 0 else ("fac",))
        spread(s, ch)

    solved = n
    for j in range(links * n):
        do_spread(j)
        if n - HELD <= j + n - HELD < n:
            first_send(j + n - HELD)
        if j + n - LAG >= n:
            do_solve(j + n - LAG)
            solved += 1
    while solved < steps * n:
        do_solve(solved)
        solved += 1

    for c in cross.values():
        c.wait_send()
    first_out.wait()
    pltpu.make_async_copy(stage.at[later, 0], out.at[later, 0, 0, :, mine], o_loc.at[0]).wait()
    give = remote(stage.at[later, 1], out.at[later, 0, 0, :, mine], o_send.at[0], o_recv.at[0], pair)
    give.wait_send()
    give.wait_recv()
    for s in range(max(0, links - 2), links):
        for ch in range(n):
            z_sent(s, ch)
    remote(sent, landed, c_send.at[0], c_recv.at[0, 0], pair).wait_send()


def on_device(n_col, n_row, rhs, diag_inv, factor, columns):
    steps, rows, width = rhs.shape[0], rhs.shape[3], rhs.shape[4]
    columns = jnp.swapaxes(columns, 3, 4)
    targets, slots = factor.shape[3], factor.shape[4]
    chips, half = n_col // 2, width // 2
    wide, links = half // CHUNKS, steps - 1
    fold = max(1, 128 // wide)
    packed = (rows // fold, wide * fold)
    bf16 = jnp.bfloat16
    dma = pltpu.SemaphoreType.DMA
    scratch = [
        pltpu.VMEM((steps, 2, rows, half), bf16),
        pltpu.VMEM((steps, 2, rows, rows), bf16),
        pltpu.VMEM((links, 2, targets, slots, rows, rows), bf16),
        pltpu.SMEM(columns.shape, jnp.int32),
        pltpu.VMEM((CHUNKS, 2, rows, wide), jnp.float32),
        pltpu.VMEM((links, CHUNKS, chips - 1, 2) + packed, bf16),
        pltpu.VMEM((links, CHUNKS, chips - 1, 2) + packed, bf16),
        pltpu.VMEM((steps, 2, rows, half), bf16),
        dma((3, 2)), dma((5,)), dma((5,)),
        dma((2, CHUNKS)), dma((2, CHUNKS)), dma((CHUNKS,)),
        dma((1,)), dma((2, CHUNKS)),
        dma((2,)), dma((1,)), dma((1,)),
        pltpu.VMEM((rows, width), bf16), pltpu.VMEM((rows, width), bf16), pltpu.VMEM((CHUNKS,) + packed, bf16),
    ] + [pltpu.VMEM((n_row, 2) + packed, bf16) for _ in range(links * CHUNKS)]
    anywhere = pl.BlockSpec(memory_space=pl.ANY)
    return pl.pallas_call(
        functools.partial(kernel, n_col, n_row),
        out_shape=jax.ShapeDtypeStruct(rhs.shape, bf16),
        in_specs=[anywhere, anywhere, anywhere, pl.BlockSpec(memory_space=pltpu.SMEM), anywhere],
        out_specs=anywhere,
        scratch_shapes=scratch,
        compiler_params=pltpu.CompilerParams(
            collective_id=0, has_side_effects=True, vmem_limit_bytes=60 * 1024 * 1024),
        name="levels",
    )(rhs, diag_inv, factor, columns, columns)


def solution(mesh):
    n_col, n_row = mesh.shape["col"], mesh.shape["row"]
    return jax.shard_map(
        functools.partial(on_device, n_col, n_row),
        mesh=mesh,
        in_specs=(
            P(None, "col", "row", None, None),
            P(None, "col", "row", None, None),
            P(None, "col", "row", None, None, None, None),
            P(None, "col", "row", None, None),
        ),
        out_specs=P(None, "col", "row", None, None),
        check_vma=False,
    )
```

```python
import functools

import jax
import jax.numpy as jnp
from jax import lax
from jax.experimental import pallas as pl
from jax.experimental.pallas import tpu as pltpu
from jax.sharding import PartitionSpec as P

MESH = pl.DeviceIdType.MESH
CHUNKS = 4
LAG = 1
HELD = 1


def kernel(n_col, n_row, rhs, diag, fac, cols, cols_hbm, out, *scratch):
    steps, rows, width = rhs.shape[0], rhs.shape[3], rhs.shape[4]
    slots = fac.shape[4]
    chips = n_col // 2
    half = width // 2
    wide = half // CHUNKS
    fold = max(1, 128 // wide)
    tall = rows // fold
    links = steps - 1

    (rv, dv, fv, cp, own, sent, landed, stage,
     in_loc, in_send, in_recv, z_send, z_recv, swapped, c_send, c_recv,
     o_loc, o_send, o_recv, first_rhs, first_sol, first_pair) = scratch[:22]
    panels = scratch[22:]

    col = lax.axis_index("col")
    row = lax.axis_index("row")
    core = lax.rem(col, 2)
    chip = lax.div(col, 2)
    partner = col + 1 - 2 * core
    mine = pl.ds(pl.multiple_of(core * half, half), half)
    theirs = pl.ds(pl.multiple_of((1 - core) * half, half), half)

    def to(c, r):
        return {"col": c, "row": r}

    def spans(total):
        return [pl.ds(0, 1), pl.ds(1, total - 1)]

    def chip_at(d):
        if chips & (chips - 1):
            return lax.rem(chip + d, chips)
        other, bit = chip, 1
        while bit < chips:
            if d & bit:
                other = other + bit - 2 * bit * lax.rem(lax.div(chip, bit), 2)
            bit *= 2
        return other

    away = sorted(range(1, chips), key=lambda d: -bin(d).count("1"))

    barrier = pltpu.get_barrier_semaphore()
    pl.semaphore_signal(barrier, inc=1, device_id=to(partner, row), device_id_type=MESH)
    for d in range(1, n_row):
        for c in (col, partner):
            pl.semaphore_signal(barrier, inc=1, device_id=to(c, lax.rem(row + d, n_row)), device_id_type=MESH)
    for d in away:
        pl.semaphore_signal(barrier, inc=1, device_id=to(chip_at(d) * 2 + core, row), device_id_type=MESH)

    local = {
        ("rhs", 0): pltpu.make_async_copy(rhs.at[0, 0, 0], first_rhs, in_loc.at[0, 0]),
        ("diag", 0): pltpu.make_async_copy(diag.at[0, 0, 0], dv.at[0, 0], in_loc.at[1, 0]),
    }
    later = pl.ds(1, steps - 1)
    for g in range(2):
        b = spans(links)[g]
        local["fac", g] = pltpu.make_async_copy(fac.at[b, 0, 0], fv.at[b, 0], in_loc.at[2, g])
        if g == 0:
            local["rhs", 1] = pltpu.make_async_copy(rhs.at[later, 0, 0, :, mine], rv.at[later, 0], in_loc.at[0, 1])
            local["diag", 1] = pltpu.make_async_copy(diag.at[later, 0, 0], dv.at[later, 0], in_loc.at[1, 1])
    for c in local.values():
        c.start()

    def pack(x):
        return x if fold == 1 else jnp.concatenate(
            [x[i * tall:(i + 1) * tall] for i in range(fold)], axis=1)

    local["rhs", 0].wait()
    local["diag", 0].wait()
    first_sol[...] = jnp.dot(dv[0, 0], first_rhs[...], preferred_element_type=jnp.float32).astype(jnp.bfloat16)
    first_out = pltpu.make_async_copy(first_sol, out.at[0, 0, 0], o_loc.at[1])
    first_out.start()
    keep, give = first_sol[:, mine], first_sol[:, theirs]
    for ch in range(CHUNKS):
        panels[ch][row, 0] = pack(keep[:, ch * wide:(ch + 1) * wide])
        first_pair[ch] = pack(give[:, ch * wide:(ch + 1) * wide])
    pl.semaphore_wait(barrier, 2 * n_row + chips - 2)

    def remote(src, dst, send, recv, device):
        return pltpu.make_async_remote_copy(
            src_ref=src, dst_ref=dst, send_sem=send, recv_sem=recv,
            device_id=device, device_id_type=MESH)

    pair = to(partner, row)
    cross = {}
    for g in range(2):
        b = spans(links)[g]
        if g == 0:
            cross["cols", 0] = remote(cols_hbm, cp, in_send.at[0], in_recv.at[0], pair)
        cross["fac", g] = remote(fac.at[b, 0, 0], fv.at[b, 1], in_send.at[1 + g], in_recv.at[1 + g], pair)
        if g == 0:
            cross["rhs", 1] = remote(rhs.at[later, 0, 0, :, theirs], rv.at[later, 1], in_send.at[3], in_recv.at[3], pair)
            cross["diag", 1] = remote(diag.at[later, 0, 0], dv.at[later, 1], in_send.at[4], in_recv.at[4], pair)

    def first_copy(ch, slot, target):
        buf = panels[ch].at[row, slot]
        if slot == 0:
            return remote(buf, buf, z_send.at[0, ch], z_recv.at[0, ch], to(col, target))
        return remote(first_pair.at[ch], buf, z_send.at[0, ch], z_recv.at[0, ch], to(partner, target))

    def first_swap(ch):
        return remote(first_pair.at[ch], panels[ch].at[row, 1], z_send.at[1, ch], swapped.at[ch], pair)

    def first_send(ch):
        for d in range(n_row - 1, 0, -1):
            for target in (row + d, row - d):
                @pl.when((target >= 0) & (target < n_row))
                def _():
                    for slot in range(2):
                        first_copy(ch, slot, target).start()
        first_swap(ch).start()

    for ch in range(CHUNKS - HELD):
        first_send(ch)
    for name, c in cross.items():
        if name != ("fac", 1):
            c.start()

    def arrived(name, g):
        if (name, g) in local:
            local[name, g].wait()
        cross[name, g].wait_recv()

    def unpack(x):
        return x if fold == 1 else jnp.concatenate(
            [x[:, i * wide:(i + 1) * wide] for i in range(fold)], axis=0)

    def part(ch):
        return pl.ds(ch * wide, wide)

    def z_copy(s, ch, source, target):
        buf = panels[s * CHUNKS + ch].at[source]
        return remote(buf, buf, z_send.at[s % 2, ch], z_recv.at[s % 2, ch], to(col, target))

    def z_sent(s, ch):
        many = panels[s * CHUNKS + ch].at[pl.ds(0, n_row - 1)]
        remote(many, many, z_send.at[s % 2, ch], z_recv.at[s % 2, ch], pair).wait_send()

    def z_own(s, ch):
        if s >= 2:
            z_sent(s - 2, ch)
        if s == 1:
            first_swap(ch).wait_send()
        for d in range(n_row - 1, 0, -1):
            for target in (row + d, row - d):
                ok = (target >= 0) & (target < n_row)

                @pl.when(ok)
                def _():
                    z_copy(s, ch, row, target).start()

    def z_wait(s, ch):
        if s == 0:
            first_swap(ch).wait_recv()
        many = panels[s * CHUNKS + ch].at[pl.ds(0, n_row - 1)]
        remote(many, many, z_send.at[s % 2, ch], z_recv.at[s % 2, ch], pair).wait_recv()

    def c_copy(s, ch, d):
        other = chip_at(d) * 2 + core
        return remote(sent.at[s, ch, d - 1], landed.at[s, ch, d - 1], c_send.at[0],
                      c_recv.at[s % 2, ch], to(other, row))

    def c_wait(s, ch):
        remote(sent.at[s, ch], landed.at[s, ch], c_send.at[0], c_recv.at[s % 2, ch], to(col, row)).wait_recv()

    def out_copies(s, ch):
        first, size = (ch + 1 - fold) * wide, fold * wide
        span = pl.ds(pl.multiple_of(core * half + first, size), size)
        src = stage.at[s, :, :, pl.ds(first, size)]
        keep = pltpu.make_async_copy(src.at[0], out.at[s, 0, 0, :, span], o_loc.at[0])
        give = remote(src.at[1], out.at[s, 0, 0, :, span], o_send.at[0], o_recv.at[0], pair)
        return keep, give

    def solve(s, ch):
        c_wait(s - 1, ch)
        for k in range(2):
            block = dv[s, k]
            right = rv[s, k, :, part(ch)]
            total = own[ch, k]
            for d in range(1, chips):
                total = total + landed[s - 1, ch, d - 1, k].astype(jnp.float32)
            rem = pack(right).astype(jnp.float32) - total
            high = rem.astype(jnp.bfloat16)
            low = (rem - high.astype(jnp.float32)).astype(jnp.bfloat16)
            x = jnp.dot(jnp.concatenate([block, block], axis=1),
                        jnp.concatenate([unpack(high), unpack(low)], axis=0),
                        preferred_element_type=jnp.float32)
            x = x.astype(jnp.bfloat16)
            if s < links:
                panels[s * CHUNKS + ch][row, k] = pack(x)
            stage[s, k, :, part(ch)] = x
        if s < links:
            z_own(s, ch)
        if ch % fold == fold - 1:
            for c in out_copies(s, ch):
                c.start()

    def term(s, ch, other, k):
        buf = panels[s * CHUNKS + ch]
        t = other * 2 + (core if k == 0 else 1 - core)
        left, right = [], []
        for slot, index in ((0, cols), (1, cp)):
            for m in range(slots):
                left.append(fv[s, slot, t, m])
                right.append(unpack(buf[index[s, 0, 0, m, t], slot]))
        return jnp.dot(jnp.concatenate(left, axis=1), jnp.concatenate(right, axis=0),
                       preferred_element_type=jnp.float32)

    def spread(s, ch):
        z_wait(s, ch)
        for d in away:
            other = chip_at(d)
            for k in range(2):
                sent[s, ch, d - 1, k] = pack(term(s, ch, other, k).astype(jnp.bfloat16))
            c_copy(s, ch, d).start()
        for k in range(2):
            own[ch, k] = pack(term(s, ch, chip, k))

    def ready(s, names):
        if s < 2:
            for name in names:
                arrived(name, s)

    n = CHUNKS

    def do_solve(i):
        s, ch = divmod(i, n)
        if ch == 0 and s == 1:
            ready(s, ("rhs", "diag"))
        solve(s, ch)

    def do_spread(j):
        s, ch = divmod(j, n)
        if ch == 0:
            ready(s, ("fac", "cols") if s == 0 else ("fac",))
        spread(s, ch)

    solved = n
    for j in range(links * n):
        do_spread(j)
        if j == 0:
            cross["fac", 1].start()
        if n - HELD <= j + n - HELD < n:
            first_send(j + n - HELD)
        if j + n - LAG >= n:
            do_solve(j + n - LAG)
            solved += 1
    while solved < steps * n:
        do_solve(solved)
        solved += 1

    for c in cross.values():
        c.wait_send()
    first_out.wait()
    pltpu.make_async_copy(stage.at[later, 0], out.at[later, 0, 0, :, mine], o_loc.at[0]).wait()
    give = remote(stage.at[later, 1], out.at[later, 0, 0, :, mine], o_send.at[0], o_recv.at[0], pair)
    give.wait_send()
    give.wait_recv()
    for s in range(max(0, links - 2), links):
        for ch in range(n):
            z_sent(s, ch)
    remote(sent, landed, c_send.at[0], c_recv.at[0, 0], pair).wait_send()


def on_device(n_col, n_row, rhs, diag_inv, factor, columns):
    steps, rows, width = rhs.shape[0], rhs.shape[3], rhs.shape[4]
    columns = jnp.swapaxes(columns, 3, 4)
    targets, slots = factor.shape[3], factor.shape[4]
    chips, half = n_col // 2, width // 2
    wide, links = half // CHUNKS, steps - 1
    fold = max(1, 128 // wide)
    packed = (rows // fold, wide * fold)
    bf16 = jnp.bfloat16
    dma = pltpu.SemaphoreType.DMA
    scratch = [
        pltpu.VMEM((steps, 2, rows, half), bf16),
        pltpu.VMEM((steps, 2, rows, rows), bf16),
        pltpu.VMEM((links, 2, targets, slots, rows, rows), bf16),
        pltpu.SMEM(columns.shape, jnp.int32),
        pltpu.VMEM((CHUNKS, 2) + packed, jnp.float32),
        pltpu.VMEM((links, CHUNKS, chips - 1, 2) + packed, bf16),
        pltpu.VMEM((links, CHUNKS, chips - 1, 2) + packed, bf16),
        pltpu.VMEM((steps, 2, rows, half), bf16),
        dma((3, 2)), dma((5,)), dma((5,)),
        dma((2, CHUNKS)), dma((2, CHUNKS)), dma((CHUNKS,)),
        dma((1,)), dma((2, CHUNKS)),
        dma((2,)), dma((1,)), dma((1,)),
        pltpu.VMEM((rows, width), bf16), pltpu.VMEM((rows, width), bf16), pltpu.VMEM((CHUNKS,) + packed, bf16),
    ] + [pltpu.VMEM((n_row, 2) + packed, bf16) for _ in range(links * CHUNKS)]
    anywhere = pl.BlockSpec(memory_space=pl.ANY)
    return pl.pallas_call(
        functools.partial(kernel, n_col, n_row),
        out_shape=jax.ShapeDtypeStruct(rhs.shape, bf16),
        in_specs=[anywhere, anywhere, anywhere, pl.BlockSpec(memory_space=pltpu.SMEM), anywhere],
        out_specs=anywhere,
        scratch_shapes=scratch,
        compiler_params=pltpu.CompilerParams(
            collective_id=0, has_side_effects=True, vmem_limit_bytes=60 * 1024 * 1024),
        name="levels",
    )(rhs, diag_inv, factor, columns, columns)


def solution(mesh):
    n_col, n_row = mesh.shape["col"], mesh.shape["row"]
    return jax.shard_map(
        functools.partial(on_device, n_col, n_row),
        mesh=mesh,
        in_specs=(
            P(None, "col", "row", None, None),
            P(None, "col", "row", None, None),
            P(None, "col", "row", None, None, None, None),
            P(None, "col", "row", None, None),
        ),
        out_specs=P(None, "col", "row", None, None),
        check_vma=False,
    )
```
